128 devices in a mesh: obs: 32 (over x, y, core), grp: 4 (over z).
Axes of the slice: x: 4, y: 4, z: 4, core: 2. Of those that a mesh axis runs over, the one named last changes fastest.
Arguments:
- design_panel: bfloat16 [65536, 512], P('obs'), may hold values from -0.0234375 to 0.0234375
- design_junction: bfloat16 [65536, 4096], P('obs'), may hold values from -0.046875 to 0.046875
- obs_weight: float32 [65536], P('obs'), may hold values from 0.25 to 4
- observed: bfloat16 [65536], P('obs'), may hold values from -6 to 6
- parent: int32 [4096], replicated, may hold values from 0 to 31, as said below
Outputs:
- parent_rows: float32 [14336, 4096], P('obs', 'grp')
- parent_rhs: float32 [14336], P('obs')
The draws below stay inside these ranges and needn't reach their ends.
Inputs may be any that keep to these rules, and one draw needn't show every extreme that they name: Among the 128 junctions j with the same j // 128, at most 14 have the same parent; one parent has exactly 14 of them in every such block.
All inputs are finite; a program needn't handle non-finite values.
Results may differ from the reference program's by a relative error of at most 0.0029.
Values sent between devices are 32-bit elements; how exact they have to be, the bound alone decides.
A program may use at most 128 MiB of HBM per device.

```python
import math
import jax
import jax.numpy as jnp
from jax import lax

NJ = 4096
PANEL = 512
ROW_DEV = 2048
ROWS = 65536
CB = 128
CAP = 14
N_OBS = 32


def design_pair(key):
    base = jax.random.fold_in(key, 7)
    key_panel, key_noise, key_index, key_mix, key_sign = jax.random.split(base, 5)
    norm_scale = ROWS ** (-0.5)
    panel = jnp.clip(jax.random.normal(key_panel, (ROWS, PANEL), jnp.float32), -6.0, 6.0)
    noise = jnp.clip(jax.random.normal(key_noise, (ROWS, NJ), jnp.float32), -6.0, 6.0)
    panel = panel * norm_scale
    noise = noise * norm_scale
    column_index = jax.random.randint(key_index, (NJ,), 0, PANEL)
    signs = jnp.where(jax.random.bernoulli(key_sign, 0.5, (NJ,)), 1.0, -1.0)
    mixing = jax.random.uniform(key_mix, (NJ,), jnp.float32, 0.4, 1.0) * signs
    junction = noise + panel[:, column_index] * mixing[None, :]
    return (panel, junction)


def draw_design_panel(key, part):
    panel, junction = design_pair(key)
    return panel.astype(jnp.bfloat16)


def draw_design_junction(key, part):
    panel, junction = design_pair(key)
    return junction.astype(jnp.bfloat16)


def draw_parent(key, part):
    base = jax.random.fold_in(key, 29)
    key_busiest, key_blocks = jax.random.split(base)
    busiest = jax.random.randint(key_busiest, (), 0, N_OBS)
    block_keys = jax.random.split(key_blocks, N_OBS)

    def one_block(block_key):
        key_pick, key_order = jax.random.split(block_key)
        chosen = jax.random.permutation(key_pick, (N_OBS - 1) * CAP)[:CB - CAP]
        others = (chosen // CAP).astype(jnp.int32)
        others = others + (others >= busiest).astype(jnp.int32)
        owners = jnp.concatenate([jnp.zeros((CAP,), jnp.int32) + busiest, others])
        order = jax.random.permutation(key_order, CB)
        return owners[order]
    return jax.vmap(one_block)(block_keys).reshape(NJ).astype(jnp.int32)


def steps_of(stream_key, shape, cuts, smallest, top_value):
    level, own = 1.0, jax.random.fold_in(stream_key, 6)
    for position, blocks in cuts:
        steps = jnp.exp(jax.random.uniform(jax.random.fold_in(own, position), (blocks,), jnp.float32, smallest / len(cuts), top_value / len(cuts)))
        level = level * jnp.repeat(steps, shape[position] // blocks).reshape([-1 if axis == position else 1 for axis in range(len(shape))])
    return level


def bell_draw(stream_key, dims, spread, reach, shards=(), kind=jnp.bfloat16):
    drawn = jax.random.normal(stream_key, dims, jnp.float32) * spread
    if len(shards) > 0:
        drawn = steps_of(stream_key, dims, shards, -0.22, 0.18) * drawn
    return jnp.clip(drawn, min=-reach, max=reach).astype(kind)


def setup_inputs(seed: int = 0) -> dict:
    streams_of = jax.random.split(jax.random.key(seed), 6)
    design_panel = draw_design_panel(jax.random.fold_in(streams_of[5], 71), 0)
    design_junction = draw_design_junction(jax.random.fold_in(streams_of[5], 71), 0)
    obs_weight = jnp.clip(jnp.exp(math.log(4.0) - 2.7725887 * jax.random.uniform(streams_of[2], (ROWS,), jnp.float32) ** steps_of(streams_of[2], (ROWS,), ((0, 32),), -0.2, 0.2)), 0.25, 4.0)
    observed = bell_draw(streams_of[3], (ROWS,), 1.0, 6.0, ((0, 32),))
    parent = draw_parent(jax.random.fold_in(streams_of[5], 71), 0)
    return {"design_panel": design_panel, "design_junction": design_junction, "obs_weight": obs_weight, "observed": observed, "parent": parent}


def reference(design_panel, design_junction, obs_weight, observed, parent):
    row_dims = (((0,), (0,)), ((), ()))
    weighted_panel = (obs_weight[:, None] * design_panel.astype(jnp.float32)).astype(jnp.bfloat16)
    weighted_obs = (obs_weight * observed.astype(jnp.float32)).astype(jnp.bfloat16)
    normal_pp = lax.dot_general(design_panel.astype(jnp.float32), weighted_panel.astype(jnp.float32), row_dims, preferred_element_type=jnp.float32)
    normal_jp = lax.dot_general(design_junction.astype(jnp.float32), weighted_panel.astype(jnp.float32), row_dims, preferred_element_type=jnp.float32)
    rhs_p = lax.dot_general(design_panel.astype(jnp.float32), weighted_obs.astype(jnp.float32), row_dims, preferred_element_type=jnp.float32)
    rhs_j = lax.dot_general(design_junction.astype(jnp.float32), weighted_obs.astype(jnp.float32), row_dims, preferred_element_type=jnp.float32)
    stacked_junction = design_junction.reshape(N_OBS, ROW_DEV, NJ)
    stacked_weight = obs_weight.reshape(N_OBS, ROW_DEV)

    def accumulate(total, inputs):
        rows_junction, rows_weight = inputs
        weighted = (rows_weight[:, None] * rows_junction.astype(jnp.float32)).astype(jnp.bfloat16)
        update = lax.dot_general(rows_junction.astype(jnp.float32), weighted.astype(jnp.float32), row_dims, preferred_element_type=jnp.float32)
        return (total + update, None)
    normal_jj, _ = lax.scan(accumulate, jnp.zeros((NJ, NJ), jnp.float32), (stacked_junction, stacked_weight))
    factor = jnp.linalg.cholesky(normal_pp)
    panel_cols = jax.scipy.linalg.solve_triangular(factor, normal_jp.T, lower=True).T
    reduced_p = jax.scipy.linalg.solve_triangular(factor, rhs_p, lower=True)
    schur = normal_jj - jnp.dot(panel_cols, panel_cols.T, precision=lax.Precision.HIGHEST)
    reduced_rhs = rhs_j - jnp.dot(panel_cols, reduced_p, precision=lax.Precision.HIGHEST)
    owner_grid = parent.reshape(N_OBS, CB)
    onehot = (owner_grid[:, :, None] == jnp.arange(N_OBS, dtype=jnp.int32)[None, None, :]).astype(jnp.int32)
    before = jnp.cumsum(onehot, axis=1) - onehot
    slot_index = jnp.sum(before * onehot, axis=2).reshape(NJ)
    source = jnp.arange(NJ, dtype=jnp.int32) // CB
    target = parent * (N_OBS * CAP) + source * CAP + slot_index
    parent_rows = jnp.zeros((N_OBS * N_OBS * CAP, NJ), jnp.float32).at[target].set(schur)
    parent_rhs = jnp.zeros((N_OBS * N_OBS * CAP,), jnp.float32).at[target].set(reduced_rhs)
    return (parent_rows, parent_rhs)
```

```python
import jax
import jax.numpy as jnp
from jax import lax
from jax.sharding import PartitionSpec as P


def contract_rows(left, right):
    return lax.dot_general(
        left, right, (((0,), (0,)), ((), ())), preferred_element_type=jnp.float32
    )


def local(design_panel, design_junction, obs_weight, observed, parent):
    obs_size = lax.axis_size("obs")
    group_size = lax.axis_size("grp")
    obs_index = lax.axis_index("obs")
    grp_index = lax.axis_index("grp")
    panel = design_panel.shape[1]
    junctions = design_junction.shape[1]
    slab_width = junctions // group_size
    block_rows = junctions // obs_size
    capacity = 3 * block_rows // obs_size + 2
    weights = obs_weight[:, None]
    weighted_panel = (weights * design_panel.astype(jnp.float32)).astype(jnp.bfloat16)
    weighted_obs = (obs_weight * observed.astype(jnp.float32)).astype(jnp.bfloat16)
    slab_start = grp_index * slab_width
    row_start = obs_index * block_rows
    slab_design = lax.dynamic_slice_in_dim(design_junction, slab_start, slab_width, 1)
    weighted_slab = (weights * slab_design.astype(jnp.float32)).astype(jnp.bfloat16)
    normal_pp = contract_rows(design_panel, weighted_panel)
    normal_jp = contract_rows(slab_design, weighted_panel)
    rhs = contract_rows(jnp.concatenate([design_panel, slab_design], axis=1), weighted_obs)
    rhs_len = rhs.shape[0]
    rhs = jnp.pad(rhs, (0, (-rhs_len) % panel)).reshape(-1, panel)
    stacked = jnp.concatenate([normal_pp, rhs], axis=0)
    stacked, normal_jp = lax.psum((stacked, normal_jp), "obs")
    normal_pp = stacked[:panel]
    rhs = stacked[panel:].reshape(-1)[:rhs_len]
    rhs_p = rhs[:panel]
    rhs_slab = rhs[panel:]
    offset = row_start % slab_width
    cand_jp = lax.dynamic_slice_in_dim(normal_jp, offset, block_rows, 0)
    cand_rhs = lax.dynamic_slice_in_dim(rhs_slab, offset, block_rows, 0)
    cand = jnp.concatenate(
        [cand_jp, cand_rhs[:, None], jnp.zeros((block_rows, 127), jnp.float32)], axis=1
    )
    gathered = lax.all_gather(cand, "grp", axis=0, tiled=False)
    jj_partial = contract_rows(design_junction, weighted_slab)
    normal_pp, _ = lax.optimization_barrier((normal_pp, jj_partial))
    gathered, jj_partial = lax.optimization_barrier((gathered, jj_partial))
    normal_block = lax.psum_scatter(jj_partial, "obs", scatter_dimension=0, tiled=True)
    mine = lax.dynamic_index_in_dim(gathered, row_start // slab_width, 0, keepdims=False)
    block_jp = mine[:, :panel]
    block_rhs = mine[:, panel]
    factor = jnp.linalg.cholesky(normal_pp)
    reduced_p = jax.scipy.linalg.solve_triangular(factor, rhs_p, lower=True)
    panel_sel = jax.scipy.linalg.solve_triangular(
        factor, jnp.concatenate([normal_jp, block_jp], axis=0).T, lower=True
    ).T
    panel_slab = panel_sel[:slab_width]
    panel_rows = panel_sel[slab_width:]
    schur_block = normal_block - jnp.dot(panel_rows, panel_slab.T, precision=lax.Precision.HIGHEST)
    rhs_rows = block_rhs - jnp.dot(panel_rows, reduced_p, precision=lax.Precision.HIGHEST)
    owners = lax.dynamic_slice_in_dim(parent, row_start, block_rows, 0)
    onehot = (owners[:, None] == jnp.arange(obs_size, dtype=jnp.int32)[None, :]).astype(jnp.int32)
    before = jnp.cumsum(onehot, axis=0) - onehot
    slot_index = jnp.sum(before * onehot, axis=1)
    target = owners * capacity + slot_index
    send_rows = (
        jnp.zeros((obs_size * capacity, slab_width), jnp.float32).at[target].set(schur_block)
    )
    send_rhs = jnp.zeros((obs_size * capacity,), jnp.float32).at[target].set(rhs_rows)
    got_rows, got_rhs = (
        lax.all_to_all(send_rows, "obs", split_axis=0, concat_axis=0, tiled=True),
        lax.all_to_all(send_rhs, "obs", split_axis=0, concat_axis=0, tiled=True),
    )
    return (got_rows, got_rhs)


def solution(mesh):
    in_specs = (P("obs", None), P("obs", None), P("obs"), P("obs"), P())
    out_specs = (P("obs", "grp"), P("obs"))
    return jax.shard_map(local, mesh=mesh, in_specs=in_specs, out_specs=out_specs, check_vma=False)
```

```python
import jax
import jax.numpy as jnp
from jax import lax
from jax.sharding import PartitionSpec as P


def contract_rows(left, right):
    return lax.dot_general(
        left, right, (((0,), (0,)), ((), ())), preferred_element_type=jnp.float32
    )


def local(design_panel, design_junction, obs_weight, observed, parent):
    obs_size = lax.axis_size("obs")
    group_size = lax.axis_size("grp")
    obs_index = lax.axis_index("obs")
    grp_index = lax.axis_index("grp")
    panel = design_panel.shape[1]
    junctions = design_junction.shape[1]
    slab_width = junctions // group_size
    block_rows = junctions // obs_size
    capacity = 3 * block_rows // obs_size + 2
    weights = obs_weight[:, None]
    weighted_panel = (weights * design_panel.astype(jnp.float32)).astype(jnp.bfloat16)
    weighted_obs = (obs_weight * observed.astype(jnp.float32)).astype(jnp.bfloat16)
    slab_start = grp_index * slab_width
    row_start = obs_index * block_rows
    slab_design = lax.dynamic_slice_in_dim(design_junction, slab_start, slab_width, 1)
    weighted_slab = (weights * slab_design.astype(jnp.float32)).astype(jnp.bfloat16)
    normal_pp = contract_rows(design_panel, weighted_panel)
    normal_jp = contract_rows(slab_design, weighted_panel)
    rhs = contract_rows(jnp.concatenate([design_panel, slab_design], axis=1), weighted_obs)
    rhs_len = rhs.shape[0]
    rhs = jnp.pad(rhs, (0, (-rhs_len) % panel)).reshape(-1, panel)
    stacked = jnp.concatenate([normal_jp, normal_pp, rhs], axis=0)
    stacked = jnp.pad(stacked, ((0, (-stacked.shape[0]) % (8 * obs_size)), (0, 0)))
    stacked = lax.psum_scatter(stacked, "obs", scatter_dimension=0, tiled=True)
    stacked = lax.all_gather(stacked, "obs", axis=0, tiled=True)
    normal_jp = stacked[:slab_width]
    stacked = stacked[slab_width:]
    normal_pp = stacked[:panel]
    rhs = stacked[panel:].reshape(-1)[:rhs_len]
    rhs_p = rhs[:panel]
    rhs_slab = rhs[panel:]
    offset = row_start % slab_width
    cand_jp = lax.dynamic_slice_in_dim(normal_jp, offset, block_rows, 0)
    cand_rhs = lax.dynamic_slice_in_dim(rhs_slab, offset, block_rows, 0)
    cand = jnp.concatenate(
        [cand_jp, cand_rhs[:, None], jnp.zeros((block_rows, 127), jnp.float32)], axis=1
    )
    gathered = lax.all_gather(cand, "grp", axis=0, tiled=False)
    jj_partial = contract_rows(design_junction, weighted_slab)
    normal_pp, _ = lax.optimization_barrier((normal_pp, jj_partial))
    gathered, jj_partial = lax.optimization_barrier((gathered, jj_partial))
    normal_block = lax.psum_scatter(jj_partial, "obs", scatter_dimension=0, tiled=True)
    mine = lax.dynamic_index_in_dim(gathered, row_start // slab_width, 0, keepdims=False)
    block_jp = mine[:, :panel]
    block_rhs = mine[:, panel]
    factor = jnp.linalg.cholesky(normal_pp)
    reduced_p = jax.scipy.linalg.solve_triangular(factor, rhs_p, lower=True)
    panel_sel = jax.scipy.linalg.solve_triangular(
        factor, jnp.concatenate([normal_jp, block_jp], axis=0).T, lower=True
    ).T
    panel_slab = panel_sel[:slab_width]
    panel_rows = panel_sel[slab_width:]
    schur_block = normal_block - jnp.dot(panel_rows, panel_slab.T, precision=lax.Precision.HIGHEST)
    rhs_rows = block_rhs - jnp.dot(panel_rows, reduced_p, precision=lax.Precision.HIGHEST)
    owners = lax.dynamic_slice_in_dim(parent, row_start, block_rows, 0)
    onehot = (owners[:, None] == jnp.arange(obs_size, dtype=jnp.int32)[None, :]).astype(jnp.int32)
    before = jnp.cumsum(onehot, axis=0) - onehot
    slot_index = jnp.sum(before * onehot, axis=1)
    target = owners * capacity + slot_index
    payload = jnp.concatenate(
        [schur_block, rhs_rows[:, None], jnp.zeros((block_rows, 127), jnp.float32)], axis=1
    )
    send = jnp.zeros((obs_size * capacity, slab_width + 128), jnp.float32).at[target].set(payload)
    got = lax.all_to_all(send, "obs", split_axis=0, concat_axis=0, tiled=True)
    return (got[:, :slab_width], got[:, slab_width])


def solution(mesh):
    in_specs = (P("obs", None), P("obs", None), P("obs"), P("obs"), P())
    out_specs = (P("obs", "grp"), P("obs"))
    return jax.shard_map(local, mesh=mesh, in_specs=in_specs, out_specs=out_specs, check_vma=False)
```
